32 devices in a mesh: grp: 2 (over x), node: 8 (over z, y), tm: 2 (over core).
Axes of the slice: x: 2, y: 2, z: 4, core: 2. Of those that a mesh axis runs over, the one named last changes fastest.
Arguments:
- scaled_kelvin: float32 [128, 8192], P(('grp', 'node', 'tm')), parts along dimension 0, may hold values from 0.5 to 1.5
- surface_emittance: float32 [16384], P('grp'), parts along dimension 0, may hold values from 0.2 to 1
- loss_factors: float32 [128, 8192], P(('grp', 'node', 'tm')), parts along dimension 0, may hold values from -6 to 6
- gebhart_tiles: bfloat16 [128, 32, 128, 128], P(('grp', 'node')), parts along dimension 0, may hold values from 1.4603138e-06 to 0.0014648438
- tile_target_index: int32 [128, 32], P(('grp', 'node')), parts along dimension 0, may hold values from 0 to 63
- tile_slots_occupied: int32 [128], P(('grp', 'node')), parts along dimension 0, may hold values from 16 to 32, as said below
Outputs:
- temp_sensitivity: float32 [128, 8192], P(('grp', 'node', 'tm')), parts along dimension 0
The draws below stay inside these ranges and needn't reach their ends.
There are 2 independent parts, one for each index of `grp`. The reference program is written for one: setup_inputs(seed, part) draws one part's arguments, and reference() takes and returns one part's arrays. A program takes and returns all parts, laid end to end along the dimension named above; each array names one. Nothing has to cross between parts.
Inputs may be any that keep to these rules, and one draw needn't show every extreme that they name: A row's slots k below tile_slots_occupied are used, the others are ignored; some row of every variant uses all 32.
All inputs are finite; a program needn't handle non-finite values.
Results may differ from the reference program's by a relative error of at most 0.0036.
Values may be sent and summed in bfloat16 or wider, within the bound.
No kernel may reach another device: no remote copies, remote signals or barrier semaphores. Data moves between devices by JAX's collectives and lax.ppermute only.
A program may use at most 192 MiB of HBM per device.

```python
import math
import jax
import jax.numpy as jnp
from jax import lax

BLOCK = 128
SLOTS = 32
NBLOCKS = 64
SURFACE_COUNT = 8192
EPOCH_COUNT = 64


def draw_tile_slots_occupied(key, part):
    key_base = jax.random.fold_in(key, 11)
    key_forced = jax.random.fold_in(key, 13)
    counted = jax.random.randint(key_base, (NBLOCKS,), SLOTS // 2, SLOTS + 1)
    forced = jax.random.randint(key_forced, (), 0, NBLOCKS)
    counted = jnp.where(jnp.arange(NBLOCKS) == forced, SLOTS, counted)
    return counted.astype(jnp.int32)


def with_ends(entries, own_key, low, high):
    spot = [jax.random.randint(jax.random.fold_in(own_key, axis), (), 0, length) for axis, length in enumerate(entries.shape)]
    main_axis = entries.shape.index(max(entries.shape))
    next_to = spot[:main_axis] + [(spot[main_axis] + 1) % entries.shape[main_axis]] + spot[main_axis + 1:]
    return entries.at[tuple(spot)].set(low).at[tuple(next_to)].set(high)


def block_levels(rng, extent, pieces, low, top_value):
    factor_of, own = 1.0, jax.random.fold_in(rng, 6)
    for dim, shards_of in pieces:
        heights = jnp.exp(jax.random.uniform(jax.random.fold_in(own, dim), (shards_of,), jnp.float32, low / len(pieces), top_value / len(pieces)))
        factor_of = factor_of * jnp.repeat(heights, extent[dim] // shards_of).reshape([-1 if axis == dim else 1 for axis in range(len(extent))])
    return factor_of


def scatter_about(rng, dims, spread, reach, pieces=(), kind=jnp.bfloat16):
    factor_of = block_levels(rng, dims, pieces, -0.22, 0.18) if pieces else 1.0
    array = jax.random.normal(rng, dims, jnp.float32) * spread * factor_of
    return jnp.minimum(jnp.maximum(array, -reach), reach).astype(kind)


def setup_inputs(seed: int = 0, part: int = 0) -> dict:
    seeds = jax.random.split(jax.random.key(seed), 7)
    own_keys = jax.random.split(jax.random.fold_in(seeds[6], part), 7)
    scaled_kelvin = jnp.clip(0.5 + 1.0 * jax.random.uniform(own_keys[0], (EPOCH_COUNT, SURFACE_COUNT), jnp.float32) ** block_levels(own_keys[0], (EPOCH_COUNT, SURFACE_COUNT), ((0, 16),), -0.2, 0.2), 0.5, 1.5)
    surface_emittance = jnp.clip(jax.random.uniform(own_keys[1], (SURFACE_COUNT,), jnp.float32, 0.2, 1.0), 0.2, 1.0)
    loss_factors = scatter_about(own_keys[2], (EPOCH_COUNT, SURFACE_COUNT), 1.0, 6.0, ((0, 16),), jnp.float32)
    gebhart_tiles = jnp.clip(jnp.exp(math.log(0.0014648438) - 6.9108525 * jax.random.uniform(own_keys[3], (NBLOCKS, SLOTS, BLOCK, BLOCK), jnp.float32) ** block_levels(own_keys[3], (NBLOCKS, SLOTS, BLOCK, BLOCK), ((0, 8),), -0.2, 0.2)), 1.4603137969970703e-06, 0.0014648438).astype(jnp.bfloat16)
    tile_target_index = with_ends(jax.random.randint(own_keys[4], (NBLOCKS, SLOTS), 0, NBLOCKS), jax.random.fold_in(own_keys[4], 1), 0, NBLOCKS - 1).astype(jnp.int32)
    tile_slots_occupied = draw_tile_slots_occupied(jax.random.fold_in(jax.random.fold_in(seeds[6], part), 71), part)
    return {"scaled_kelvin": scaled_kelvin, "surface_emittance": surface_emittance, "loss_factors": loss_factors, "gebhart_tiles": gebhart_tiles, "tile_target_index": tile_target_index, "tile_slots_occupied": tile_slots_occupied}


def reference(scaled_kelvin, surface_emittance, loss_factors, gebhart_tiles, tile_target_index, tile_slots_occupied):
    radiant_output = (surface_emittance[None, :] * scaled_kelvin ** 4).astype(jnp.bfloat16)
    emit_wide = radiant_output.astype(jnp.float32)
    epoch_range = scaled_kelvin.shape[0]
    panel_view = emit_wide.reshape(epoch_range, NBLOCKS, BLOCK)
    in_use = jnp.arange(SLOTS, dtype=jnp.int32)[None, :] < tile_slots_occupied[:, None]

    def row_flux(operands):
        tiles, columns, usable = operands
        picked = jnp.take(panel_view, columns, axis=1) * usable.astype(jnp.float32)[None, :, None]
        return jnp.einsum("tkj,kij->ti", picked, tiles.astype(jnp.float32))

    flux = lax.map(row_flux, (gebhart_tiles, tile_target_index, in_use))
    flux = flux.transpose(1, 0, 2).reshape(epoch_range, SURFACE_COUNT)
    weight = loss_factors * (flux - emit_wide)
    rounded = lax.optimization_barrier(weight.astype(jnp.bfloat16)).astype(jnp.float32)
    weight_rows = rounded.reshape(epoch_range, NBLOCKS, BLOCK).transpose(1, 0, 2)

    def add_row(collected, operands):
        tiles, columns, usable, weight_row = operands
        contrib = jnp.einsum("ti,kij->tkj", weight_row, tiles.astype(jnp.float32))
        targets = jnp.where(usable, columns, NBLOCKS)
        return collected.at[:, targets, :].add(contrib, mode="drop"), None

    start_sum = jnp.zeros((epoch_range, NBLOCKS, BLOCK), jnp.float32)
    collected, unused = lax.scan(add_row, start_sum, (gebhart_tiles, tile_target_index, in_use, weight_rows))
    costate_vector = collected.reshape(epoch_range, SURFACE_COUNT) - weight
    return 4.0 * surface_emittance[None, :] * scaled_kelvin ** 3 * costate_vector
```

```python
import functools

import jax
import jax.numpy as jnp
from jax import lax
from jax.experimental import pallas as pl
from jax.experimental.pallas import tpu as pltpu
from jax.sharding import PartitionSpec as P


def adjoint_kernel(
    peers, epochs, group, own_ref, target_ref, occupied_ref, *refs
):
    emit_refs = refs[:peers]
    loss_refs = refs[peers : 2 * peers]
    tile_ref = refs[2 * peers]
    out_refs = refs[2 * peers + 1 : 3 * peers + 1]
    emission, collected = refs[3 * peers + 1 :]
    row, rows = pl.program_id(0), pl.num_programs(0)
    blocks_all = emission.shape[0] - 1
    side = emission.shape[2]
    slots = tile_ref.shape[1]

    @pl.when(row == 0)
    def _():
        @pl.loop(0, blocks_all // 4)
        def _(quad):
            start = pl.multiple_of(quad * 4 * epochs, 4 * epochs)
            parts = [ref[pl.ds(start, 4 * epochs), :].astype(jnp.float32) for ref in emit_refs]
            for c in range(4):
                emission[quad * 4 + c] = jnp.concatenate(
                    [part[c * epochs : (c + 1) * epochs] for part in parts], 0
                ).astype(jnp.bfloat16)

        emission[blocks_all] = jnp.zeros(emission.shape[1:], jnp.bfloat16)
        collected[...] = jnp.zeros_like(collected)

    occupied = occupied_ref[row]
    columns = [jnp.where(k < occupied, target_ref[row, k], blocks_all) for k in range(slots)]
    flux = jnp.zeros(emission.shape[1:], jnp.float32)
    for first in range(0, slots, group):
        span = range(first, first + group)
        picked = jnp.concatenate([emission[columns[k]] for k in span], 1)
        tiles = jnp.concatenate([tile_ref[0, k] for k in span], 1)
        flux += lax.dot_general(
            picked, tiles, (((1,), (1,)), ((), ())), preferred_element_type=jnp.float32
        )
    own = own_ref[0] + row
    loss = jnp.concatenate([ref[row] for ref in loss_refs], 0)
    weight = loss * (flux - emission[own].astype(jnp.float32))
    weight_b = weight.astype(jnp.bfloat16)
    collected[own] -= weight
    for first in range(0, slots, group):
        tiles = jnp.concatenate([tile_ref[0, k] for k in range(first, first + group)], 1)
        terms = jnp.dot(weight_b, tiles, preferred_element_type=jnp.float32)
        for k in range(group):
            collected[columns[first + k]] += terms[:, k * side : (k + 1) * side]

    @pl.when(row == rows - 1)
    def _():
        @pl.loop(0, blocks_all // 4)
        def _(quad):
            start = pl.multiple_of(quad * 4 * epochs, 4 * epochs)
            parts = [collected[quad * 4 + c] for c in range(4)]
            for p, ref in enumerate(out_refs):
                ref[pl.ds(start, 4 * epochs), :] = jnp.concatenate(
                    [part[p * epochs : (p + 1) * epochs] for part in parts], 0
                ).astype(jnp.bfloat16)


def adjoint_terms(own_start, targets, occupied, emit_pieces, loss_pieces, tiles):
    peers = len(emit_pieces)
    rows, slots, side = tiles.shape[:3]
    piece_rows = emit_pieces[0].shape[0]
    epochs = loss_pieces[0].shape[1]
    blocks_all = piece_rows // epochs
    samples = peers * epochs
    resident = pl.BlockSpec(memory_space=pltpu.VMEM)
    need = (
        (blocks_all + 1) * samples * side * 6
        + 2 * peers * piece_rows * side * 2
        + 4 * slots * side * side
        + peers * rows * 8 * side * 4
    )
    return pl.pallas_call(
        functools.partial(adjoint_kernel, peers, epochs, min(8, slots)),
        grid_spec=pltpu.PrefetchScalarGridSpec(
            num_scalar_prefetch=3,
            grid=(rows,),
            in_specs=[resident] * (2 * peers)
            + [pl.BlockSpec((1, slots, side, side), lambda r, *_: (r, 0, 0, 0))],
            out_specs=[resident] * peers,
            scratch_shapes=[
                pltpu.VMEM((blocks_all + 1, samples, side), jnp.bfloat16),
                pltpu.VMEM((blocks_all + 1, samples, side), jnp.float32),
            ],
        ),
        out_shape=[jax.ShapeDtypeStruct((piece_rows, side), jnp.bfloat16)] * peers,
        compiler_params=pltpu.CompilerParams(vmem_limit_bytes=need + (6 << 20)),
        cost_estimate=pl.CostEstimate(
            flops=4 * rows * slots * side * side * samples,
            bytes_accessed=rows * slots * side * side * 2,
            transcendentals=0,
        ),
    )(own_start, targets, occupied, *emit_pieces, *loss_pieces, tiles)


def on_device(
    nodes,
    scaled_kelvin,
    surface_emittance,
    loss_factors,
    gebhart_tiles,
    tile_target_index,
    tile_slots_occupied,
):
    rows, side = gebhart_tiles.shape[0], gebhart_tiles.shape[2]
    epochs, surfaces = scaled_kelvin.shape
    blocks_all = surfaces // side
    me = lax.axis_index("node")

    def send(value, step):
        return lax.ppermute(value, "node", [(i, i ^ step) for i in range(nodes)])

    def by_block(value):
        return value.reshape(-1, blocks_all, side).transpose(1, 0, 2)

    kelvin = by_block(scaled_kelvin)
    emittance = surface_emittance.reshape(blocks_all, 1, side)
    emission = (emittance * kelvin**4).astype(jnp.bfloat16).reshape(blocks_all * epochs, side)
    loss = by_block(loss_factors).reshape(nodes, rows, epochs, side)
    loss = lax.all_to_all(loss, "node", split_axis=0, concat_axis=0, tiled=True)
    loss_pieces = [lax.dynamic_index_in_dim(loss, me ^ p, 0, False) for p in range(nodes)]

    far = range(nodes - 2, 0, -2)
    emit = {0: emission}
    for p in far:
        emit[p] = send(emission, p)
    emit[1] = send(emission, 1)
    for p in far:
        emit[p ^ 1] = send(emit[p], 1)

    terms = adjoint_terms(
        (me * rows).astype(jnp.int32)[None],
        tile_target_index,
        tile_slots_occupied,
        [emit[p] for p in range(nodes)],
        loss_pieces,
        gebhart_tiles,
    )

    arrived = {p: send(terms[p ^ 1], 1) for p in [*far, 0]}
    paired = {p: terms[p].astype(jnp.float32) + arrived[p].astype(jnp.float32) for p in [*far, 0]}
    total = paired[0]
    for p in far:
        total += send(paired[p].astype(jnp.bfloat16), p).astype(jnp.float32)
    adjoint = total.reshape(blocks_all, epochs, side)
    result = 4.0 * emittance * kelvin**3 * adjoint
    return result.transpose(1, 0, 2).reshape(epochs, surfaces)


def solution(mesh):
    nodes = mesh.shape["node"]
    assert nodes & (nodes - 1) == 0
    placed = (
        P(("grp", "node", "tm"), None),
        P("grp"),
        P(("grp", "node", "tm"), None),
        P(("grp", "node"), None, None, None),
        P(("grp", "node"), None),
        P(("grp", "node")),
    )
    return jax.shard_map(
        functools.partial(on_device, nodes),
        mesh=mesh,
        in_specs=placed,
        out_specs=P(("grp", "node", "tm"), None),
        check_vma=False,
    )
```

```python
import functools

import jax
import jax.numpy as jnp
from jax import lax
from jax.experimental import pallas as pl
from jax.experimental.pallas import tpu as pltpu
from jax.sharding import PartitionSpec as P

RESIDENT = pl.BlockSpec(memory_space=pltpu.VMEM)
F32, BF16 = jnp.float32, jnp.bfloat16


def halves(value):
    high = value.astype(BF16)
    return high, (value - high.astype(F32)).astype(BF16)


def prepare_kernel(
    far, rows, kelvin_ref, emittance_ref, loss_ref, target_ref, occupied_ref, *out_refs
):
    z_refs = out_refs[: len(far)]
    own_ref, pair_ref, scale_ref, table_ref = out_refs[len(far) :]
    epochs = kelvin_ref.shape[0]
    blocks_all, side = emittance_ref.shape
    me = lax.axis_index("node")
    part = rows * epochs
    wide = blocks_all * epochs

    for first in range(0, blocks_all, 4):
        emissions, scales = [], []
        for c in range(first, first + 4):
            kelvin = kelvin_ref[:, c * side : (c + 1) * side]
            emittance = emittance_ref[c : c + 1, :]
            square = kelvin * kelvin
            emissions.append(emittance * (square * square))
            scales.append(4.0 * emittance * (square * kelvin))
        emission = jnp.concatenate(emissions, 0).astype(BF16)
        span = slice(first * epochs, (first + 4) * epochs)
        scale_ref[span, :] = jnp.concatenate(scales, 0)
        own_ref[span, :] = emission
        pair_ref[span, :] = emission
        for ref in z_refs:
            ref[2 * part + first * epochs : 2 * part + (first + 4) * epochs, :] = emission

    def put_loss(ref, start, peer):
        width = rows * side
        loss = loss_ref[:, pl.ds(pl.multiple_of(peer * width, width), width)]
        loss = jnp.concatenate([loss[:, r * side : (r + 1) * side] for r in range(rows)], 0)
        high, low = halves(loss)
        ref[start : start + part, :] = high
        ref[start + part : start + 2 * part, :] = low

    put_loss(own_ref, wide, me)
    put_loss(pair_ref, wide, me ^ 1)
    for p, ref in zip(far, z_refs):
        put_loss(ref, 0, me ^ p)
        put_loss(ref, 2 * part + wide, me ^ p ^ 1)

    slots = target_ref.shape[1]
    slot = lax.broadcasted_iota(jnp.int32, (1, slots), 1)
    for r in range(rows):
        table_ref[r : r + 1, :] = jnp.where(
            slot < occupied_ref[r], target_ref[r : r + 1, :], blocks_all
        )


def prepare(far, scaled_kelvin, surface_emittance, loss_factors, targets, occupied, side):
    epochs, surfaces = scaled_kelvin.shape
    rows = targets.shape[0]
    blocks_all = surfaces // side
    part, wide = 2 * rows * epochs, blocks_all * epochs
    held = [
        pltpu.with_memory_space_constraint(value, pltpu.HBM)
        for value in (
            scaled_kelvin,
            surface_emittance.reshape(blocks_all, side),
            loss_factors,
            targets,
            occupied,
        )
    ]
    whole = lambda value: pl.BlockSpec(value.shape, lambda i: (0,) * value.ndim)
    return pl.pallas_call(
        functools.partial(prepare_kernel, far, rows),
        grid=(1,),
        in_specs=[whole(value) for value in held[:4]] + [pl.BlockSpec(memory_space=pltpu.SMEM)],
        out_specs=[RESIDENT] * (len(far) + 4),
        out_shape=[jax.ShapeDtypeStruct((wide + 2 * part, side), BF16)] * len(far)
        + [jax.ShapeDtypeStruct((wide + part, side), BF16)] * 2
        + [jax.ShapeDtypeStruct((wide, side), F32), jax.ShapeDtypeStruct(targets.shape, jnp.int32)],
        compiler_params=pltpu.CompilerParams(vmem_limit_bytes=24 << 20),
    )(*held)


def adjoint_kernel(peers, rows, epochs, group, table_ref, *refs):
    piece_refs, tiles_ref = refs[:peers], refs[peers]
    out_refs = refs[peers + 1 : 2 * peers + 1]
    tiles, emission, loss, collected, sems = refs[2 * peers + 1 :]
    blocks_all, samples, side = emission.shape[0] - 1, emission.shape[1], emission.shape[2]
    slots = tiles.shape[1]
    part, wide = rows * epochs, blocks_all * epochs
    me = lax.axis_index("node")

    loads = [pltpu.make_async_copy(tiles_ref.at[r], tiles.at[r], sems.at[r]) for r in range(rows)]
    for load in loads:
        load.start()

    emit_at = [2 * part if p and not p & 1 else 0 for p in range(peers)]
    loss_at = [0 if p and not p & 1 else wide for p in range(peers)]

    @pl.loop(0, blocks_all // 4)
    def _(quad):
        step = pl.multiple_of(quad * 4 * epochs, 4 * epochs)
        parts = [
            ref[pl.ds(start + step, 4 * epochs), :].astype(F32)
            for ref, start in zip(piece_refs, emit_at)
        ]
        for c in range(4):
            emission[quad * 4 + c] = jnp.concatenate(
                [part[c * epochs : (c + 1) * epochs] for part in parts], 0
            ).astype(BF16)

    for first in range(0, rows, 4):
        parts = []
        for ref, start in zip(piece_refs, loss_at):
            span = slice(start + first * epochs, start + (first + 4) * epochs)
            rest = slice(span.start + part, span.stop + part)
            parts.append(ref[span, :].astype(F32) + ref[rest, :].astype(F32))
        for c in range(4):
            loss[first + c] = jnp.concatenate(
                [value[c * epochs : (c + 1) * epochs] for value in parts], 0
            )

    emission[blocks_all] = jnp.zeros(emission.shape[1:], BF16)
    collected[...] = jnp.zeros_like(collected)

    for block_rows in [range(first, first + 4) for first in range(0, rows, 4)]:
        for r in block_rows:
            loads[r].wait()
        weights = {}
        for r in block_rows:
            flux = jnp.zeros((samples, side), F32)
            for first in range(0, slots, group):
                span = range(first, first + group)
                picked = jnp.concatenate([emission[table_ref[r, k]] for k in span], 1)
                stored = jnp.concatenate([tiles[r, k] for k in span], 1)
                flux += lax.dot_general(
                    picked, stored, (((1,), (1,)), ((), ())), preferred_element_type=F32
                )
            own = me * rows + r
            weight = loss[r] * (flux - emission[own].astype(F32))
            weights[r] = weight.astype(BF16)
            collected[own] -= weight
        for r in block_rows:
            for first in range(0, slots, group):
                stored = jnp.concatenate([tiles[r, k] for k in range(first, first + group)], 1)
                terms = jnp.dot(weights[r], stored, preferred_element_type=F32)
                for k in range(group):
                    collected[table_ref[r, first + k]] += terms[:, k * side : (k + 1) * side]

    @pl.loop(0, blocks_all // 4)
    def _(quad):
        step = pl.multiple_of(quad * 4 * epochs, 4 * epochs)
        parts = [collected[quad * 4 + c] for c in range(4)]
        for p, ref in enumerate(out_refs):
            ref[pl.ds(step, 4 * epochs), :] = jnp.concatenate(
                [part[p * epochs : (p + 1) * epochs] for part in parts], 0
            ).astype(BF16)

    for first in range(0, rows, 4):
        parts = [collected[me * rows + first + c] for c in range(4)]
        for p, ref in enumerate(out_refs):
            full = jnp.concatenate([part[p * epochs : (p + 1) * epochs] for part in parts], 0)
            ref[wide + first * epochs : wide + (first + 4) * epochs, :] = halves(full)[1]


def adjoint_terms(table, pieces, tiles, epochs, blocks_all):
    peers = len(pieces)
    rows, slots, side = tiles.shape[:3]
    samples = peers * epochs
    out_rows = (blocks_all + rows) * epochs
    need = (
        (blocks_all + 1) * samples * side * 6
        + 2 * peers * out_rows * side * 2
        + rows * slots * side * side * 2
        + rows * samples * side * 4
    )
    return pl.pallas_call(
        functools.partial(adjoint_kernel, peers, rows, epochs, min(8, slots)),
        in_specs=[pl.BlockSpec(memory_space=pltpu.SMEM)]
        + [RESIDENT] * peers
        + [pl.BlockSpec(memory_space=pl.ANY)],
        out_specs=[RESIDENT] * peers,
        scratch_shapes=[
            pltpu.VMEM(tiles.shape, BF16),
            pltpu.VMEM((blocks_all + 1, samples, side), BF16),
            pltpu.VMEM((rows, samples, side), F32),
            pltpu.VMEM((blocks_all + 1, samples, side), F32),
            pltpu.SemaphoreType.DMA((rows,)),
        ],
        out_shape=[jax.ShapeDtypeStruct((out_rows, side), BF16)] * peers,
        compiler_params=pltpu.CompilerParams(vmem_limit_bytes=need + (6 << 20)),
        cost_estimate=pl.CostEstimate(
            flops=4 * rows * slots * side * side * samples,
            bytes_accessed=rows * slots * side * side * 2,
            transcendentals=0,
        ),
    )(table, *pieces, pltpu.with_memory_space_constraint(tiles, pltpu.HBM))


def finish_kernel(steps, rows, epochs, scale_ref, *refs):
    sum_refs, out_ref, total = refs[: len(steps)], refs[-2], refs[-1]
    wide, side = total.shape
    part = 2 * rows * epochs
    pair = lax.axis_index("node") // 2
    total[...] = sum(ref[:wide, :].astype(F32) for ref in sum_refs)
    for p, ref in zip(steps, sum_refs):
        span = pl.ds(pl.multiple_of((pair ^ (p // 2)) * part, part), part)
        total[span, :] += ref[wide:, :].astype(F32)
    for c in range(wide // epochs):
        span = slice(c * epochs, (c + 1) * epochs)
        out_ref[:, c * side : (c + 1) * side] = scale_ref[span, :] * total[span, :]


def finish(steps, rows, epochs, scale, sums):
    wide, side = scale.shape
    return pl.pallas_call(
        functools.partial(finish_kernel, steps, rows, epochs),
        in_specs=[RESIDENT] * (1 + len(sums)),
        out_specs=RESIDENT,
        scratch_shapes=[pltpu.VMEM((wide, side), F32)],
        out_shape=jax.ShapeDtypeStruct((epochs, wide // epochs * side), F32),
        compiler_params=pltpu.CompilerParams(vmem_limit_bytes=24 << 20),
    )(scale, *sums)


def add_neighbour(me, wide, mine, theirs):
    total = mine[:wide].astype(F32) + theirs[:wide].astype(F32)
    low_mine, low_theirs = mine[wide:].astype(F32), theirs[wide:].astype(F32)
    odd = me % 2 == 1
    low = jnp.concatenate(
        [jnp.where(odd, low_theirs, low_mine), jnp.where(odd, low_mine, low_theirs)], 0
    )
    start = (me // 2) * low.shape[0]
    high, low = halves(lax.dynamic_slice_in_dim(total, start, low.shape[0], 0) + low)
    total = lax.dynamic_update_slice_in_dim(total.astype(BF16), high, start, 0)
    return jnp.concatenate([total, low], 0)


def on_device(
    nodes,
    scaled_kelvin,
    surface_emittance,
    loss_factors,
    gebhart_tiles,
    tile_target_index,
    tile_slots_occupied,
):
    rows, side = gebhart_tiles.shape[0], gebhart_tiles.shape[2]
    epochs, surfaces = scaled_kelvin.shape
    blocks_all = surfaces // side
    wide = blocks_all * epochs
    me = lax.axis_index("node")

    def send(value, step):
        return lax.ppermute(value, "node", [(i, i ^ step) for i in range(nodes)])

    far = tuple(range(nodes - 2, 0, -2))
    *along_z, own, pair, scale, table = prepare(
        far,
        scaled_kelvin,
        surface_emittance,
        loss_factors,
        tile_target_index,
        tile_slots_occupied,
        side,
    )
    pieces = {0: own}
    for p, piece in zip(far, along_z):
        pieces[p] = send(piece, p)
    pieces[1] = send(pair, 1)
    for p in far:
        pieces[p ^ 1] = send(pieces[p][2 * rows * epochs :], 1)

    terms = adjoint_terms(
        table, [pieces[p] for p in range(nodes)], gebhart_tiles, epochs, blocks_all
    )

    steps = (*far, 0)
    arrived = {p: send(terms[p ^ 1], 1) for p in steps}
    paired = {p: add_neighbour(me, wide, terms[p], arrived[p]) for p in steps}
    sums = [send(paired[p], p) for p in far] + [paired[0]]
    return finish(steps, rows, epochs, scale, sums)


def solution(mesh):
    nodes = mesh.shape["node"]
    assert nodes & (nodes - 1) == 0
    placed = (
        P(("grp", "node", "tm"), None),
        P("grp"),
        P(("grp", "node", "tm"), None),
        P(("grp", "node"), None, None, None),
        P(("grp", "node"), None),
        P(("grp", "node")),
    )
    return jax.shard_map(
        functools.partial(on_device, nodes),
        mesh=mesh,
        in_specs=placed,
        out_specs=P(("grp", "node", "tm"), None),
        check_vma=False,
    )
```

```python
import functools

import jax
import jax.numpy as jnp
from jax import lax
from jax.experimental import pallas as pl
from jax.experimental.pallas import tpu as pltpu
from jax.sharding import PartitionSpec as P

RESIDENT = pl.BlockSpec(memory_space=pltpu.VMEM)
F32, BF16 = jnp.float32, jnp.bfloat16


def halves(value):
    high = value.astype(BF16)
    return high, (value - high.astype(F32)).astype(BF16)


def prepare_kernel(
    far, rows, kelvin_ref, emittance_ref, loss_ref, target_ref, occupied_ref, *out_refs
):
    z_refs = out_refs[: len(far)]
    own_ref, pair_ref, scale_ref, table_ref = out_refs[len(far) :]
    epochs = kelvin_ref.shape[0]
    blocks_all, side = emittance_ref.shape
    me = lax.axis_index("node")
    part = rows * epochs
    wide = blocks_all * epochs

    for first in range(0, blocks_all, 4):
        emissions, scales = [], []
        for c in range(first, first + 4):
            kelvin = kelvin_ref[:, c * side : (c + 1) * side]
            emittance = emittance_ref[c : c + 1, :]
            square = kelvin * kelvin
            emissions.append(emittance * (square * square))
            scales.append(4.0 * emittance * (square * kelvin))
        emission = jnp.concatenate(emissions, 0).astype(BF16)
        span = slice(first * epochs, (first + 4) * epochs)
        scale_ref[span, :] = jnp.concatenate(scales, 0)
        own_ref[span, :] = emission
        pair_ref[span, :] = emission
        for ref in z_refs:
            ref[2 * part + first * epochs : 2 * part + (first + 4) * epochs, :] = emission

    def put_loss(ref, start, peer):
        width = rows * side
        loss = loss_ref[:, pl.ds(pl.multiple_of(peer * width, width), width)]
        loss = jnp.concatenate([loss[:, r * side : (r + 1) * side] for r in range(rows)], 0)
        high, low = halves(loss)
        ref[start : start + part, :] = high
        ref[start + part : start + 2 * part, :] = low

    put_loss(own_ref, wide, me)
    put_loss(pair_ref, wide, me ^ 1)
    for p, ref in zip(far, z_refs):
        put_loss(ref, 0, me ^ p)
        put_loss(ref, 2 * part + wide, me ^ p ^ 1)

    slots = target_ref.shape[1]
    slot = lax.broadcasted_iota(jnp.int32, (1, slots), 1)
    for r in range(rows):
        table_ref[r : r + 1, :] = jnp.where(
            slot < occupied_ref[r], target_ref[r : r + 1, :], blocks_all
        )


def prepare(far, scaled_kelvin, surface_emittance, loss_factors, targets, occupied, side):
    epochs, surfaces = scaled_kelvin.shape
    rows = targets.shape[0]
    blocks_all = surfaces // side
    part, wide = 2 * rows * epochs, blocks_all * epochs
    held = [
        pltpu.with_memory_space_constraint(value, pltpu.HBM)
        for value in (
            scaled_kelvin,
            surface_emittance.reshape(blocks_all, side),
            loss_factors,
            targets,
            occupied,
        )
    ]
    whole = lambda value: pl.BlockSpec(value.shape, lambda i: (0,) * value.ndim)
    return pl.pallas_call(
        functools.partial(prepare_kernel, far, rows),
        grid=(1,),
        in_specs=[whole(value) for value in held[:4]] + [pl.BlockSpec(memory_space=pltpu.SMEM)],
        out_specs=[RESIDENT] * (len(far) + 4),
        out_shape=[jax.ShapeDtypeStruct((wide + 2 * part, side), BF16)] * len(far)
        + [jax.ShapeDtypeStruct((wide + part, side), BF16)] * 2
        + [jax.ShapeDtypeStruct((wide, side), F32), jax.ShapeDtypeStruct(targets.shape, jnp.int32)],
        compiler_params=pltpu.CompilerParams(vmem_limit_bytes=24 << 20),
    )(*held)


def load_kernel(after_ref, tiles_ref, out_ref, sems):
    loads = [
        pltpu.make_async_copy(tiles_ref.at[r], out_ref.at[r], sems.at[r])
        for r in range(out_ref.shape[0])
    ]
    for load in loads:
        load.start()
    for load in loads:
        load.wait()


def load_tiles(tiles, after, rows):
    return pl.pallas_call(
        load_kernel,
        in_specs=[pl.BlockSpec(memory_space=pl.ANY)] * 2,
        out_specs=RESIDENT,
        scratch_shapes=[pltpu.SemaphoreType.DMA((rows,))],
        out_shape=jax.ShapeDtypeStruct((rows, *tiles.shape[1:]), tiles.dtype),
        compiler_params=pltpu.CompilerParams(vmem_limit_bytes=2 * tiles.size + (1 << 20)),
        cost_estimate=pl.CostEstimate(
            flops=0, bytes_accessed=4 * tiles.size, transcendentals=0
        ),
    )(after, tiles)


def adjoint_kernel(order, rows, epochs, group, table_ref, *refs):
    peers = len(order)
    piece_refs = [refs[order.index(p)] for p in range(peers)]
    early_ref, tiles_ref = refs[peers : peers + 2]
    out_refs = refs[peers + 2 : 2 * peers + 2]
    late_ref, emission, loss, collected, sems = refs[2 * peers + 2 :]
    blocks_all, samples, side = emission.shape[0] - 1, emission.shape[1], emission.shape[2]
    early, slots = early_ref.shape[:2]
    loads = [
        pltpu.make_async_copy(tiles_ref.at[early + r], late_ref.at[r], sems.at[r])
        for r in range(rows - early)
    ]
    for load in loads:
        load.start()

    def stored_tiles(r, span):
        ref, r = (early_ref, r) if r < early else (late_ref, r - early)
        return jnp.concatenate([ref[r, k] for k in span], 1)

    part, wide = rows * epochs, blocks_all * epochs
    me = lax.axis_index("node")

    emit_at = [2 * part if p and not p & 1 else 0 for p in range(peers)]
    loss_at = [0 if p and not p & 1 else wide for p in range(peers)]

    @pl.loop(0, blocks_all // 4)
    def _(quad):
        step = pl.multiple_of(quad * 4 * epochs, 4 * epochs)
        parts = [
            ref[pl.ds(start + step, 4 * epochs), :].astype(F32)
            for ref, start in zip(piece_refs, emit_at)
        ]
        for c in range(4):
            emission[quad * 4 + c] = jnp.concatenate(
                [part[c * epochs : (c + 1) * epochs] for part in parts], 0
            ).astype(BF16)

    for first in range(0, rows, 4):
        parts = []
        for ref, start in zip(piece_refs, loss_at):
            span = slice(start + first * epochs, start + (first + 4) * epochs)
            rest = slice(span.start + part, span.stop + part)
            parts.append(ref[span, :].astype(F32) + ref[rest, :].astype(F32))
        for c in range(4):
            loss[first + c] = jnp.concatenate(
                [value[c * epochs : (c + 1) * epochs] for value in parts], 0
            )

    emission[blocks_all] = jnp.zeros(emission.shape[1:], BF16)
    collected[...] = jnp.zeros_like(collected)

    def find_weight(r):
        flux = jnp.zeros((samples, side), F32)
        for first in range(0, slots, group):
            span = range(first, first + group)
            picked = jnp.concatenate([emission[table_ref[r, k]] for k in span], 1)
            stored = stored_tiles(r, span)
            part = lax.dot_general(
                stored, picked, (((1,), (1,)), ((), ())), preferred_element_type=F32
            )
            flux = part if first == 0 else flux + part
        flux = flux.T
        own = me * rows + r
        weight = loss[r] * (flux - emission[own].astype(F32))
        collected[own] -= weight
        return weight.astype(BF16)

    def add_terms(r, weight):
        for first in range(0, slots, group):
            stored = stored_tiles(r, range(first, first + group))
            terms = jnp.dot(weight, stored, preferred_element_type=F32)
            for k in range(group):
                collected[table_ref[r, first + k]] += terms[:, k * side : (k + 1) * side]

    for block_rows in (range(early), range(early, rows)):
        for r in block_rows:
            if r >= early:
                loads[r - early].wait()
        weights = [find_weight(r) for r in block_rows]
        for r, weight in zip(block_rows, weights):
            add_terms(r, weight)

    @pl.loop(0, blocks_all // 4)
    def _(quad):
        step = pl.multiple_of(quad * 4 * epochs, 4 * epochs)
        parts = [collected[quad * 4 + c] for c in range(4)]
        for p, ref in enumerate(out_refs):
            ref[pl.ds(step, 4 * epochs), :] = jnp.concatenate(
                [part[p * epochs : (p + 1) * epochs] for part in parts], 0
            ).astype(BF16)

    for first in range(0, rows, 4):
        parts = [collected[me * rows + first + c] for c in range(4)]
        for p, ref in enumerate(out_refs):
            full = jnp.concatenate([part[p * epochs : (p + 1) * epochs] for part in parts], 0)
            ref[wide + first * epochs : wide + (first + 4) * epochs, :] = halves(full)[1]


def adjoint_terms(table, order, pieces, early, tiles, epochs, blocks_all):
    peers = len(pieces)
    rows, slots, side = tiles.shape[:3]
    samples = peers * epochs
    out_rows = (blocks_all + rows) * epochs
    need = (
        (blocks_all + 1) * samples * side * 6
        + rows * slots * side * side * 2
        + 2 * peers * out_rows * side * 2
        + rows * samples * side * 4
    )
    return pl.pallas_call(
        functools.partial(adjoint_kernel, order, rows, epochs, min(8, slots)),
        in_specs=[pl.BlockSpec(memory_space=pltpu.SMEM)]
        + [RESIDENT] * (peers + 1)
        + [pl.BlockSpec(memory_space=pl.ANY)],
        out_specs=[RESIDENT] * peers,
        scratch_shapes=[
            pltpu.VMEM((rows - early.shape[0], *tiles.shape[1:]), BF16),
            pltpu.VMEM((blocks_all + 1, samples, side), BF16),
            pltpu.VMEM((rows, samples, side), F32),
            pltpu.VMEM((blocks_all + 1, samples, side), F32),
            pltpu.SemaphoreType.DMA((rows - early.shape[0],)),
        ],
        out_shape=[jax.ShapeDtypeStruct((out_rows, side), BF16)] * peers,
        compiler_params=pltpu.CompilerParams(vmem_limit_bytes=need + (6 << 20)),
        cost_estimate=pl.CostEstimate(
            flops=4 * rows * slots * side * side * samples,
            bytes_accessed=rows * slots * side * side * 2,
            transcendentals=0,
        ),
    )(table, *[pieces[p] for p in order], early, tiles)


def finish_kernel(steps, rows, epochs, scale_ref, *refs):
    sum_refs, out_ref, total = refs[: len(steps)], refs[-2], refs[-1]
    wide, side = total.shape
    part = 2 * rows * epochs
    pair = lax.axis_index("node") // 2
    total[...] = sum(ref[:wide, :].astype(F32) for ref in sum_refs)
    for p, ref in zip(steps, sum_refs):
        span = pl.ds(pl.multiple_of((pair ^ (p // 2)) * part, part), part)
        total[span, :] += ref[wide:, :].astype(F32)
    for c in range(wide // epochs):
        span = slice(c * epochs, (c + 1) * epochs)
        out_ref[:, c * side : (c + 1) * side] = scale_ref[span, :] * total[span, :]


def finish(steps, rows, epochs, scale, sums):
    wide, side = scale.shape
    return pl.pallas_call(
        functools.partial(finish_kernel, steps, rows, epochs),
        in_specs=[RESIDENT] * (1 + len(sums)),
        out_specs=RESIDENT,
        scratch_shapes=[pltpu.VMEM((wide, side), F32)],
        out_shape=jax.ShapeDtypeStruct((epochs, wide // epochs * side), F32),
        compiler_params=pltpu.CompilerParams(vmem_limit_bytes=24 << 20),
    )(scale, *sums)


def add_neighbour(me, wide, mine, theirs):
    total = mine[:wide].astype(F32) + theirs[:wide].astype(F32)
    low_mine, low_theirs = mine[wide:].astype(F32), theirs[wide:].astype(F32)
    odd = me % 2 == 1
    low = jnp.concatenate(
        [jnp.where(odd, low_theirs, low_mine), jnp.where(odd, low_mine, low_theirs)], 0
    )
    start = (me // 2) * low.shape[0]
    window = lax.dynamic_slice_in_dim(total, start, low.shape[0], 0) + low
    high = lax.reduce_precision(window, 8, 7)
    total = lax.dynamic_update_slice_in_dim(total.astype(BF16), high.astype(BF16), start, 0)
    return jnp.concatenate([total, (window - high).astype(BF16)], 0)


def on_device(
    nodes,
    scaled_kelvin,
    surface_emittance,
    loss_factors,
    gebhart_tiles,
    tile_target_index,
    tile_slots_occupied,
):
    rows, side = gebhart_tiles.shape[0], gebhart_tiles.shape[2]
    epochs, surfaces = scaled_kelvin.shape
    blocks_all = surfaces // side
    wide = blocks_all * epochs
    me = lax.axis_index("node")

    def send(value, step):
        return lax.ppermute(value, "node", [(i, i ^ step) for i in range(nodes)])

    far = tuple(range(nodes - 2, 0, -2))
    *along_z, own, pair, scale, table = prepare(
        far,
        scaled_kelvin,
        surface_emittance,
        loss_factors,
        tile_target_index,
        tile_slots_occupied,
        side,
    )
    pieces = {0: own}
    for p, piece in zip(far, along_z):
        pieces[p] = send(piece, p)
    pieces[1] = send(pair, 1)
    for p in far:
        pieces[p ^ 1] = send(pieces[p][2 * rows * epochs :], 1)

    near = [nodes // 2 - 1, *([1] if nodes > 4 else []), *range(nodes // 2 - 2, 1, -1), 0]
    order = tuple(q for d in near for q in (2 * d + 1, 2 * d))
    tiles = pltpu.with_memory_space_constraint(gebhart_tiles, pltpu.HBM)
    early = load_tiles(tiles, pieces[far[0]], rows // 2)
    terms = adjoint_terms(table, order, pieces, early, tiles, epochs, blocks_all)

    steps = tuple(range(0, nodes, 2))
    arrived = {p: send(terms[p ^ 1], 1) for p in steps}
    paired = {p: add_neighbour(me, wide, terms[p], arrived[p]) for p in steps}
    sums = [paired[0]] + [send(paired[p], p) for p in steps[1:]]
    return finish(steps, rows, epochs, scale, sums)


def solution(mesh):
    nodes = mesh.shape["node"]
    assert nodes & (nodes - 1) == 0
    placed = (
        P(("grp", "node", "tm"), None),
        P("grp"),
        P(("grp", "node", "tm"), None),
        P(("grp", "node"), None, None, None),
        P(("grp", "node"), None),
        P(("grp", "node")),
    )
    return jax.shard_map(
        functools.partial(on_device, nodes),
        mesh=mesh,
        in_specs=placed,
        out_specs=P(("grp", "node", "tm"), None),
        check_vma=False,
    )
```

```python
import functools

import jax
import jax.numpy as jnp
from jax import lax
from jax.experimental import pallas as pl
from jax.experimental.pallas import tpu as pltpu
from jax.sharding import PartitionSpec as P

RESIDENT = pl.BlockSpec(memory_space=pltpu.VMEM)
F32, BF16 = jnp.float32, jnp.bfloat16


def halves(value):
    high = value.astype(BF16)
    return high, (value - high.astype(F32)).astype(BF16)


def prepare_kernel(
    far, rows, kelvin_ref, emittance_ref, loss_ref, target_ref, occupied_ref, *out_refs
):
    z_refs = out_refs[: len(far)]
    own_ref, pair_ref, scale_ref, table_ref = out_refs[len(far) :]
    epochs = kelvin_ref.shape[0]
    blocks_all, side = emittance_ref.shape
    me = lax.axis_index("node")
    part = rows * epochs
    wide = blocks_all * epochs

    for first in range(0, blocks_all, 4):
        emissions, scales = [], []
        for c in range(first, first + 4):
            kelvin = kelvin_ref[:, c * side : (c + 1) * side]
            emittance = emittance_ref[c : c + 1, :]
            square = kelvin * kelvin
            emissions.append(emittance * (square * square))
            scales.append(4.0 * emittance * (square * kelvin))
        emission = jnp.concatenate(emissions, 0).astype(BF16)
        span = slice(first * epochs, (first + 4) * epochs)
        scale_ref[span, :] = jnp.concatenate(scales, 0)
        own_ref[span, :] = emission
        pair_ref[span, :] = emission
        for ref in z_refs:
            ref[2 * part + first * epochs : 2 * part + (first + 4) * epochs, :] = emission

    def put_loss(ref, start, peer):
        width = rows * side
        loss = loss_ref[:, pl.ds(pl.multiple_of(peer * width, width), width)]
        loss = jnp.concatenate([loss[:, r * side : (r + 1) * side] for r in range(rows)], 0)
        high, low = halves(loss)
        ref[start : start + part, :] = high
        ref[start + part : start + 2 * part, :] = low

    put_loss(own_ref, wide, me)
    put_loss(pair_ref, wide, me ^ 1)
    for p, ref in zip(far, z_refs):
        put_loss(ref, 0, me ^ p)
        put_loss(ref, 2 * part + wide, me ^ p ^ 1)

    slots = target_ref.shape[1]
    slot = lax.broadcasted_iota(jnp.int32, (1, slots), 1)
    for r in range(rows):
        table_ref[r : r + 1, :] = jnp.where(
            slot < occupied_ref[r], target_ref[r : r + 1, :], blocks_all
        )


def prepare(far, scaled_kelvin, surface_emittance, loss_factors, targets, occupied, side):
    epochs, surfaces = scaled_kelvin.shape
    rows = targets.shape[0]
    blocks_all = surfaces // side
    part, wide = 2 * rows * epochs, blocks_all * epochs
    held = [
        pltpu.with_memory_space_constraint(value, pltpu.HBM)
        for value in (
            scaled_kelvin,
            surface_emittance.reshape(blocks_all, side),
            loss_factors,
            targets,
            occupied,
        )
    ]
    whole = lambda value: pl.BlockSpec(value.shape, lambda i: (0,) * value.ndim)
    return pl.pallas_call(
        functools.partial(prepare_kernel, far, rows),
        grid=(1,),
        in_specs=[whole(value) for value in held[:4]] + [pl.BlockSpec(memory_space=pltpu.SMEM)],
        out_specs=[RESIDENT] * (len(far) + 4),
        out_shape=[jax.ShapeDtypeStruct((wide + 2 * part, side), BF16)] * len(far)
        + [jax.ShapeDtypeStruct((wide + part, side), BF16)] * 2
        + [jax.ShapeDtypeStruct((wide, side), F32), jax.ShapeDtypeStruct(targets.shape, jnp.int32)],
        compiler_params=pltpu.CompilerParams(vmem_limit_bytes=24 << 20),
    )(*held)


def load_kernel(after_ref, tiles_ref, out_ref, sems):
    loads = [
        pltpu.make_async_copy(tiles_ref.at[r], out_ref.at[r], sems.at[r])
        for r in range(out_ref.shape[0])
    ]
    for load in loads:
        load.start()
    for load in loads:
        load.wait()


def load_tiles(tiles, after, rows):
    return pl.pallas_call(
        load_kernel,
        in_specs=[pl.BlockSpec(memory_space=pl.ANY)] * 2,
        out_specs=RESIDENT,
        scratch_shapes=[pltpu.SemaphoreType.DMA((rows,))],
        out_shape=jax.ShapeDtypeStruct((rows, *tiles.shape[1:]), tiles.dtype),
        compiler_params=pltpu.CompilerParams(vmem_limit_bytes=2 * tiles.size + (1 << 20)),
        cost_estimate=pl.CostEstimate(
            flops=0, bytes_accessed=4 * tiles.size, transcendentals=0
        ),
    )(after, tiles)


def adjoint_kernel(order, packs, rows, epochs, group, table_ref, *refs):
    peers = len(order)
    piece_refs = [refs[order.index(p)] for p in range(peers)]
    early_ref, tiles_ref = refs[peers : peers + 2]
    out_refs = refs[peers + 2 : peers + 2 + len(packs)]
    late_ref, emission, loss, collected, sems = refs[peers + 2 + len(packs) :]
    blocks_all, samples, side = emission.shape[0] - 1, emission.shape[1], emission.shape[2]
    out_rows = (blocks_all + rows) * epochs
    outs = [
        (p, ref, place * out_rows)
        for pack, ref in zip(packs, out_refs)
        for place, p in enumerate(pack)
    ]
    early, slots = early_ref.shape[:2]
    loads = [
        pltpu.make_async_copy(tiles_ref.at[early + r], late_ref.at[r], sems.at[r])
        for r in range(rows - early)
    ]
    for load in loads:
        load.start()

    def stored_tiles(r, span):
        ref, r = (early_ref, r) if r < early else (late_ref, r - early)
        return jnp.concatenate([ref[r, k] for k in span], 1)

    part, wide = rows * epochs, blocks_all * epochs
    me = lax.axis_index("node")

    emit_at = [2 * part if p and not p & 1 else 0 for p in range(peers)]
    loss_at = [0 if p and not p & 1 else wide for p in range(peers)]

    @pl.loop(0, blocks_all // 4)
    def _(quad):
        step = pl.multiple_of(quad * 4 * epochs, 4 * epochs)
        parts = [
            ref[pl.ds(start + step, 4 * epochs), :].astype(F32)
            for ref, start in zip(piece_refs, emit_at)
        ]
        for c in range(4):
            emission[quad * 4 + c] = jnp.concatenate(
                [part[c * epochs : (c + 1) * epochs] for part in parts], 0
            ).astype(BF16)

    for first in range(0, rows, 4):
        parts = []
        for ref, start in zip(piece_refs, loss_at):
            span = slice(start + first * epochs, start + (first + 4) * epochs)
            rest = slice(span.start + part, span.stop + part)
            parts.append(ref[span, :].astype(F32) + ref[rest, :].astype(F32))
        for c in range(4):
            loss[first + c] = jnp.concatenate(
                [value[c * epochs : (c + 1) * epochs] for value in parts], 0
            )

    emission[blocks_all] = jnp.zeros(emission.shape[1:], BF16)
    collected[...] = jnp.zeros_like(collected)

    def find_weight(r):
        flux = jnp.zeros((samples, side), F32)
        for first in range(0, slots, group):
            span = range(first, first + group)
            picked = jnp.concatenate([emission[table_ref[r, k]] for k in span], 1)
            stored = stored_tiles(r, span)
            part = lax.dot_general(
                stored, picked, (((1,), (1,)), ((), ())), preferred_element_type=F32
            )
            flux = part if first == 0 else flux + part
        flux = flux.T
        own = me * rows + r
        weight = loss[r] * (flux - emission[own].astype(F32))
        collected[own] -= weight
        return weight.astype(BF16)

    def add_terms(r, weight):
        for first in range(0, slots, group):
            stored = stored_tiles(r, range(first, first + group))
            terms = jnp.dot(weight, stored, preferred_element_type=F32)
            for k in range(group):
                collected[table_ref[r, first + k]] += terms[:, k * side : (k + 1) * side]

    for block_rows in (range(early), range(early, rows)):
        for r in block_rows:
            if r >= early:
                loads[r - early].wait()
        weights = [find_weight(r) for r in block_rows]
        for r, weight in zip(block_rows, weights):
            add_terms(r, weight)

    @pl.loop(0, blocks_all // 4)
    def _(quad):
        step = pl.multiple_of(quad * 4 * epochs, 4 * epochs)
        parts = [collected[quad * 4 + c] for c in range(4)]
        for p, ref, base in outs:
            ref[pl.ds(base + step, 4 * epochs), :] = jnp.concatenate(
                [part[p * epochs : (p + 1) * epochs] for part in parts], 0
            ).astype(BF16)

    for first in range(0, rows, 4):
        parts = [collected[me * rows + first + c] for c in range(4)]
        for p, ref, base in outs:
            full = jnp.concatenate([part[p * epochs : (p + 1) * epochs] for part in parts], 0)
            base += wide + first * epochs
            ref[base : base + 4 * epochs, :] = halves(full)[1]


def adjoint_terms(table, order, packs, pieces, early, tiles, epochs, blocks_all):
    peers = len(pieces)
    rows, slots, side = tiles.shape[:3]
    samples = peers * epochs
    out_rows = (blocks_all + rows) * epochs
    need = (
        (blocks_all + 1) * samples * side * 6
        + rows * slots * side * side * 2
        + 2 * peers * out_rows * side * 2
        + rows * samples * side * 4
    )
    return pl.pallas_call(
        functools.partial(adjoint_kernel, order, packs, rows, epochs, min(8, slots)),
        in_specs=[pl.BlockSpec(memory_space=pltpu.SMEM)]
        + [RESIDENT] * (peers + 1)
        + [pl.BlockSpec(memory_space=pl.ANY)],
        out_specs=[RESIDENT] * len(packs),
        scratch_shapes=[
            pltpu.VMEM((rows - early.shape[0], *tiles.shape[1:]), BF16),
            pltpu.VMEM((blocks_all + 1, samples, side), BF16),
            pltpu.VMEM((rows, samples, side), F32),
            pltpu.VMEM((blocks_all + 1, samples, side), F32),
            pltpu.SemaphoreType.DMA((rows - early.shape[0],)),
        ],
        out_shape=[jax.ShapeDtypeStruct((out_rows * len(pack), side), BF16) for pack in packs],
        compiler_params=pltpu.CompilerParams(vmem_limit_bytes=need + (6 << 20)),
        cost_estimate=pl.CostEstimate(
            flops=4 * rows * slots * side * side * samples,
            bytes_accessed=rows * slots * side * side * 2,
            transcendentals=0,
        ),
    )(table, *[pieces[p] for p in order], early, tiles)


def finish_kernel(owners, rows, epochs, scale_ref, *refs):
    sum_refs, out_ref, total = refs[: len(owners)], refs[-2], refs[-1]
    wide, side = total.shape
    part = rows * epochs
    me = lax.axis_index("node")
    total[...] = sum(ref[:wide, :].astype(F32) for ref in sum_refs)
    for steps, ref in zip(owners, sum_refs):
        for place, step in enumerate(steps):
            span = pl.ds(pl.multiple_of((me ^ step) * part, part), part)
            start = wide + place * part
            total[span, :] += ref[start : start + part, :].astype(F32)
    for c in range(wide // epochs):
        span = slice(c * epochs, (c + 1) * epochs)
        out_ref[:, c * side : (c + 1) * side] = scale_ref[span, :] * total[span, :]


def finish(owners, rows, epochs, scale, sums):
    wide, side = scale.shape
    return pl.pallas_call(
        functools.partial(finish_kernel, owners, rows, epochs),
        in_specs=[RESIDENT] * (1 + len(sums)),
        out_specs=RESIDENT,
        scratch_shapes=[pltpu.VMEM((wide, side), F32)],
        out_shape=jax.ShapeDtypeStruct((epochs, wide // epochs * side), F32),
        compiler_params=pltpu.CompilerParams(vmem_limit_bytes=24 << 20),
    )(scale, *sums)


def add_terms_of(node, other, wide, mine, theirs):
    part = mine.shape[0] - wide
    total = mine[:wide].astype(F32) + theirs[:wide].astype(F32)
    rounded, rest = total.astype(BF16), []
    for owner, low in ((node, mine[wide:]), (other, theirs[wide:])):
        window = lax.dynamic_slice_in_dim(total, owner * part, part, 0) + low.astype(F32)
        high = lax.reduce_precision(window, 8, 7)
        rounded = lax.dynamic_update_slice_in_dim(rounded, high.astype(BF16), owner * part, 0)
        rest.append((window - high).astype(BF16))
    return jnp.concatenate([rounded, *rest], 0)


def on_device(
    nodes,
    scaled_kelvin,
    surface_emittance,
    loss_factors,
    gebhart_tiles,
    tile_target_index,
    tile_slots_occupied,
):
    rows, side = gebhart_tiles.shape[0], gebhart_tiles.shape[2]
    epochs, surfaces = scaled_kelvin.shape
    blocks_all = surfaces // side
    wide = blocks_all * epochs
    me = lax.axis_index("node")

    def send(value, step):
        return lax.ppermute(value, "node", [(i, i ^ step) for i in range(nodes)])

    far = tuple(range(nodes - 2, 0, -2))
    *along_z, own, pair, scale, table = prepare(
        far,
        scaled_kelvin,
        surface_emittance,
        loss_factors,
        tile_target_index,
        tile_slots_occupied,
        side,
    )
    pieces = {0: own}
    for p, piece in zip(far, along_z):
        pieces[p] = send(piece, p)
    pieces[1] = send(pair, 1)
    for p in far:
        pieces[p ^ 1] = send(pieces[p][2 * rows * epochs :], 1)

    near = [nodes // 2 - 1, *([1] if nodes > 4 else []), *range(nodes // 2 - 2, 1, -1), 0]
    order = tuple(q for d in near for q in (2 * d + 1, 2 * d))
    tiles = pltpu.with_memory_space_constraint(gebhart_tiles, pltpu.HBM)
    early = load_tiles(tiles, pieces[far[0]], rows // 2)
    distant = range(4, nodes, 2)
    packs = (*((p,) for p in (*distant, *(p + 1 for p in distant), 0, 1)), (2, 3))
    terms = adjoint_terms(table, order, packs, pieces, early, tiles, epochs, blocks_all)
    terms = dict(zip(packs, terms))

    def add(step, mine, theirs):
        return add_terms_of(me, me ^ step, wide, mine, theirs)

    arrived = {p: send(terms[(p + 1,)], 1) for p in distant}
    near = jnp.split(send(terms[(2, 3)], 2), 2)
    sums = {p: send(add(1, terms[(p,)], arrived[p]), p) for p in distant}
    sums[1] = send(add(2, terms[(1,)], near[1]), 1)
    sums[0] = add(2, terms[(0,)], near[0])
    steps = (*distant, 1, 0)
    owners = {p: (p, p ^ 2 if p < 2 else p ^ 1) for p in steps}
    return finish(
        [owners[p] for p in steps], rows, epochs, scale, [sums[p] for p in steps]
    )


def solution(mesh):
    nodes = mesh.shape["node"]
    assert nodes & (nodes - 1) == 0
    placed = (
        P(("grp", "node", "tm"), None),
        P("grp"),
        P(("grp", "node", "tm"), None),
        P(("grp", "node"), None, None, None),
        P(("grp", "node"), None),
        P(("grp", "node")),
    )
    return jax.shard_map(
        functools.partial(on_device, nodes),
        mesh=mesh,
        in_specs=placed,
        out_specs=P(("grp", "node", "tm"), None),
        check_vma=False,
    )
```

```python
import functools

import jax
import jax.numpy as jnp
from jax import lax
from jax.experimental import pallas as pl
from jax.experimental.pallas import tpu as pltpu
from jax.sharding import PartitionSpec as P

RESIDENT = pl.BlockSpec(memory_space=pltpu.VMEM)
F32, BF16 = jnp.float32, jnp.bfloat16


def halves(value):
    high = value.astype(BF16)
    return high, (value - high.astype(F32)).astype(BF16)


def prepare_kernel(
    far, rows, kelvin_ref, emittance_ref, loss_ref, target_ref, occupied_ref, *out_refs
):
    z_refs = out_refs[: len(far)]
    own_ref, pair_ref, scale_ref, table_ref = out_refs[len(far) :]
    epochs = kelvin_ref.shape[0]
    blocks_all, side = emittance_ref.shape
    me = lax.axis_index("node")
    part = rows * epochs
    wide = blocks_all * epochs

    for first in range(0, blocks_all, 4):
        emissions, scales = [], []
        for c in range(first, first + 4):
            kelvin = kelvin_ref[:, c * side : (c + 1) * side]
            emittance = emittance_ref[c : c + 1, :]
            square = kelvin * kelvin
            emissions.append(emittance * (square * square))
            scales.append(4.0 * emittance * (square * kelvin))
        emission = jnp.concatenate(emissions, 0).astype(BF16)
        span = slice(first * epochs, (first + 4) * epochs)
        scale_ref[span, :] = jnp.concatenate(scales, 0)
        own_ref[span, :] = emission
        pair_ref[span, :] = emission
        for ref in z_refs:
            ref[2 * part + first * epochs : 2 * part + (first + 4) * epochs, :] = emission

    def put_loss(ref, start, peer):
        width = rows * side
        loss = loss_ref[:, pl.ds(pl.multiple_of(peer * width, width), width)]
        loss = jnp.concatenate([loss[:, r * side : (r + 1) * side] for r in range(rows)], 0)
        high, low = halves(loss)
        ref[start : start + part, :] = high
        ref[start + part : start + 2 * part, :] = low

    put_loss(own_ref, wide, me)
    put_loss(pair_ref, wide, me ^ 1)
    for p, ref in zip(far, z_refs):
        put_loss(ref, 0, me ^ p)
        put_loss(ref, 2 * part + wide, me ^ p ^ 1)

    slots = target_ref.shape[1]
    slot = lax.broadcasted_iota(jnp.int32, (1, slots), 1)
    for r in range(rows):
        table_ref[r : r + 1, :] = jnp.where(
            slot < occupied_ref[r], target_ref[r : r + 1, :], blocks_all
        )


def prepare(far, scaled_kelvin, surface_emittance, loss_factors, targets, occupied, side):
    epochs, surfaces = scaled_kelvin.shape
    rows = targets.shape[0]
    blocks_all = surfaces // side
    part, wide = 2 * rows * epochs, blocks_all * epochs
    held = [
        pltpu.with_memory_space_constraint(value, pltpu.HBM)
        for value in (
            scaled_kelvin,
            surface_emittance.reshape(blocks_all, side),
            loss_factors,
            targets,
            occupied,
        )
    ]
    whole = lambda value: pl.BlockSpec(value.shape, lambda i: (0,) * value.ndim)
    return pl.pallas_call(
        functools.partial(prepare_kernel, far, rows),
        grid=(1,),
        in_specs=[whole(value) for value in held[:4]] + [pl.BlockSpec(memory_space=pltpu.SMEM)],
        out_specs=[RESIDENT] * (len(far) + 4),
        out_shape=[jax.ShapeDtypeStruct((wide + 2 * part, side), BF16)] * len(far)
        + [jax.ShapeDtypeStruct((wide + part, side), BF16)] * 2
        + [jax.ShapeDtypeStruct((wide, side), F32), jax.ShapeDtypeStruct(targets.shape, jnp.int32)],
        compiler_params=pltpu.CompilerParams(vmem_limit_bytes=24 << 20),
    )(*held)


def load_kernel(after_ref, tiles_ref, out_ref, sems):
    loads = [
        pltpu.make_async_copy(tiles_ref.at[r], out_ref.at[r], sems.at[r])
        for r in range(out_ref.shape[0])
    ]
    for load in loads:
        load.start()
    for load in loads:
        load.wait()


def load_tiles(tiles, after, rows):
    return pl.pallas_call(
        load_kernel,
        in_specs=[pl.BlockSpec(memory_space=pl.ANY)] * 2,
        out_specs=RESIDENT,
        scratch_shapes=[pltpu.SemaphoreType.DMA((rows,))],
        out_shape=jax.ShapeDtypeStruct((rows, *tiles.shape[1:]), tiles.dtype),
        compiler_params=pltpu.CompilerParams(vmem_limit_bytes=2 * tiles.size + (1 << 20)),
        cost_estimate=pl.CostEstimate(
            flops=0, bytes_accessed=4 * tiles.size, transcendentals=0
        ),
    )(after, tiles)


def adjoint_kernel(order, packs, rows, epochs, group, table_ref, *refs):
    peers = len(order)
    piece_refs = [refs[order.index(p)] for p in range(peers)]
    early_ref, tiles_ref = refs[peers : peers + 2]
    out_refs = refs[peers + 2 : peers + 2 + len(packs)]
    late_ref, emission, loss, collected, sems = refs[peers + 2 + len(packs) :]
    blocks_all, samples, side = emission.shape[0] - 1, emission.shape[1], emission.shape[2]
    out_rows = (blocks_all + rows) * epochs
    outs = [
        (p, ref, place * out_rows)
        for pack, ref in zip(packs, out_refs)
        for place, p in enumerate(pack)
    ]
    early, slots = early_ref.shape[:2]
    loads = [
        pltpu.make_async_copy(tiles_ref.at[early + r], late_ref.at[r], sems.at[r])
        for r in range(rows - early)
    ]
    for load in loads:
        load.start()

    def stored_tiles(r, span):
        ref, r = (early_ref, r) if r < early else (late_ref, r - early)
        return jnp.concatenate([ref[r, k] for k in span], 1)

    part, wide = rows * epochs, blocks_all * epochs
    me = lax.axis_index("node")

    emit_at = [2 * part if p and not p & 1 else 0 for p in range(peers)]
    loss_at = [0 if p and not p & 1 else wide for p in range(peers)]

    @pl.loop(0, blocks_all // 4)
    def _(quad):
        step = pl.multiple_of(quad * 4 * epochs, 4 * epochs)
        parts = [
            ref[pl.ds(start + step, 4 * epochs), :].astype(F32)
            for ref, start in zip(piece_refs, emit_at)
        ]
        for c in range(4):
            emission[quad * 4 + c] = jnp.concatenate(
                [part[c * epochs : (c + 1) * epochs] for part in parts], 0
            ).astype(BF16)

    for first in range(0, rows, 4):
        parts = []
        for ref, start in zip(piece_refs, loss_at):
            span = slice(start + first * epochs, start + (first + 4) * epochs)
            rest = slice(span.start + part, span.stop + part)
            parts.append(ref[span, :].astype(F32) + ref[rest, :].astype(F32))
        for c in range(4):
            loss[first + c] = jnp.concatenate(
                [value[c * epochs : (c + 1) * epochs] for value in parts], 0
            )

    emission[blocks_all] = jnp.zeros(emission.shape[1:], BF16)
    collected[...] = jnp.zeros_like(collected)

    def find_weight(r):
        flux = jnp.zeros((samples, side), F32)
        for first in range(0, slots, group):
            span = range(first, first + group)
            picked = jnp.concatenate([emission[table_ref[r, k]] for k in span], 1)
            stored = stored_tiles(r, span)
            part = lax.dot_general(
                stored, picked, (((1,), (1,)), ((), ())), preferred_element_type=F32
            )
            flux = part if first == 0 else flux + part
        flux = flux.T
        own = me * rows + r
        weight = loss[r] * (flux - emission[own].astype(F32))
        collected[own] -= weight
        return weight.astype(BF16)

    def add_terms(r, weight):
        for first in range(0, slots, group):
            stored = stored_tiles(r, range(first, first + group))
            terms = jnp.dot(weight, stored, preferred_element_type=F32)
            for k in range(group):
                collected[table_ref[r, first + k]] += terms[:, k * side : (k + 1) * side]

    for block_rows in (range(early), range(early, rows)):
        for r in block_rows:
            if r >= early:
                loads[r - early].wait()
        weights = [find_weight(r) for r in block_rows]
        for r, weight in zip(block_rows, weights):
            add_terms(r, weight)

    @pl.loop(0, blocks_all // 4)
    def _(quad):
        step = pl.multiple_of(quad * 4 * epochs, 4 * epochs)
        parts = [collected[quad * 4 + c] for c in range(4)]
        for p, ref, base in outs:
            ref[pl.ds(base + step, 4 * epochs), :] = jnp.concatenate(
                [part[p * epochs : (p + 1) * epochs] for part in parts], 0
            ).astype(BF16)

    for first in range(0, rows, 4):
        parts = [collected[me * rows + first + c] for c in range(4)]
        for p, ref, base in outs:
            full = jnp.concatenate([part[p * epochs : (p + 1) * epochs] for part in parts], 0)
            base += wide + first * epochs
            ref[base : base + 4 * epochs, :] = halves(full)[1]


def adjoint_terms(table, order, packs, pieces, early, tiles, epochs, blocks_all):
    peers = len(pieces)
    rows, slots, side = tiles.shape[:3]
    samples = peers * epochs
    out_rows = (blocks_all + rows) * epochs
    need = (
        (blocks_all + 1) * samples * side * 6
        + rows * slots * side * side * 2
        + 2 * peers * out_rows * side * 2
        + rows * samples * side * 4
    )
    return pl.pallas_call(
        functools.partial(adjoint_kernel, order, packs, rows, epochs, min(8, slots)),
        in_specs=[pl.BlockSpec(memory_space=pltpu.SMEM)]
        + [RESIDENT] * (peers + 1)
        + [pl.BlockSpec(memory_space=pl.ANY)],
        out_specs=[RESIDENT] * len(packs),
        scratch_shapes=[
            pltpu.VMEM((rows - early.shape[0], *tiles.shape[1:]), BF16),
            pltpu.VMEM((blocks_all + 1, samples, side), BF16),
            pltpu.VMEM((rows, samples, side), F32),
            pltpu.VMEM((blocks_all + 1, samples, side), F32),
            pltpu.SemaphoreType.DMA((rows - early.shape[0],)),
        ],
        out_shape=[jax.ShapeDtypeStruct((out_rows * len(pack), side), BF16) for pack in packs],
        compiler_params=pltpu.CompilerParams(vmem_limit_bytes=need + (6 << 20)),
        cost_estimate=pl.CostEstimate(
            flops=4 * rows * slots * side * side * samples,
            bytes_accessed=rows * slots * side * side * 2,
            transcendentals=0,
        ),
    )(table, *[pieces[p] for p in order], early, tiles)


def finish_kernel(owners, rows, epochs, scale_ref, *refs):
    sum_refs = refs[: len(owners)]
    out_ref, total, result, sems = refs[len(owners) :]
    wide, side = total.shape
    part = rows * epochs
    me = lax.axis_index("node")
    total[...] = sum(ref[:wide, :].astype(F32) for ref in sum_refs)
    for steps, ref in zip(owners, sum_refs):
        for place, step in enumerate(steps):
            span = pl.ds(pl.multiple_of((me ^ step) * part, part), part)
            start = wide + place * part
            total[span, :] += ref[start : start + part, :].astype(F32)
    blocks_all, copies = wide // epochs, []
    for first in range(0, blocks_all, blocks_all // 4):
        for c in range(first, first + blocks_all // 4):
            span = slice(c * epochs, (c + 1) * epochs)
            result[:, c * side : (c + 1) * side] = scale_ref[span, :] * total[span, :]
        part = slice(first * side, (first + blocks_all // 4) * side)
        copies.append(
            pltpu.make_async_copy(result.at[:, part], out_ref.at[:, part], sems.at[len(copies)])
        )
        copies[-1].start()
    for copy in copies:
        copy.wait()


def finish(owners, rows, epochs, scale, sums):
    wide, side = scale.shape
    return pl.pallas_call(
        functools.partial(finish_kernel, owners, rows, epochs),
        in_specs=[RESIDENT] * (1 + len(sums)),
        out_specs=pl.BlockSpec(memory_space=pl.ANY),
        scratch_shapes=[
            pltpu.VMEM((wide, side), F32),
            pltpu.VMEM((epochs, wide // epochs * side), F32),
            pltpu.SemaphoreType.DMA((4,)),
        ],
        out_shape=jax.ShapeDtypeStruct((epochs, wide // epochs * side), F32),
        compiler_params=pltpu.CompilerParams(vmem_limit_bytes=24 << 20),
    )(scale, *sums)


def add_terms_of(node, other, wide, mine, theirs):
    part = mine.shape[0] - wide
    total = mine[:wide].astype(F32) + theirs[:wide].astype(F32)
    rounded, rest = total.astype(BF16), []
    for owner, low in ((node, mine[wide:]), (other, theirs[wide:])):
        window = lax.dynamic_slice_in_dim(total, owner * part, part, 0) + low.astype(F32)
        high = lax.reduce_precision(window, 8, 7)
        rounded = lax.dynamic_update_slice_in_dim(rounded, high.astype(BF16), owner * part, 0)
        rest.append((window - high).astype(BF16))
    return jnp.concatenate([rounded, *rest], 0)


def on_device(
    nodes,
    scaled_kelvin,
    surface_emittance,
    loss_factors,
    gebhart_tiles,
    tile_target_index,
    tile_slots_occupied,
):
    rows, side = gebhart_tiles.shape[0], gebhart_tiles.shape[2]
    epochs, surfaces = scaled_kelvin.shape
    blocks_all = surfaces // side
    wide = blocks_all * epochs
    me = lax.axis_index("node")

    def send(value, step):
        return lax.ppermute(value, "node", [(i, i ^ step) for i in range(nodes)])

    far = tuple(range(nodes - 2, 0, -2))
    *along_z, own, pair, scale, table = prepare(
        far,
        scaled_kelvin,
        surface_emittance,
        loss_factors,
        tile_target_index,
        tile_slots_occupied,
        side,
    )
    pieces = {0: own}
    for p, piece in zip(far, along_z):
        pieces[p] = send(piece, p)
    pieces[1] = send(pair, 1)
    for p in far:
        pieces[p ^ 1] = send(pieces[p][2 * rows * epochs :], 1)

    near = [nodes // 2 - 1, *([1] if nodes > 4 else []), *range(nodes // 2 - 2, 1, -1), 0]
    order = tuple(q for d in near for q in (2 * d + 1, 2 * d))
    tiles = pltpu.with_memory_space_constraint(gebhart_tiles, pltpu.HBM)
    early = load_tiles(tiles, pieces[far[0]], rows // 2)
    distant = range(4, nodes, 2)
    packs = (*((p,) for p in (*distant, *(p + 1 for p in distant), 0, 1)), (2, 3))
    terms = adjoint_terms(table, order, packs, pieces, early, tiles, epochs, blocks_all)
    terms = dict(zip(packs, terms))

    def add(step, mine, theirs):
        return add_terms_of(me, me ^ step, wide, mine, theirs)

    arrived = {p: send(terms[(p + 1,)], 1) for p in distant}
    near = jnp.split(send(terms[(2, 3)], 2), 2)
    sums = {p: send(add(1, terms[(p,)], arrived[p]), p) for p in distant}
    sums[1] = send(add(2, terms[(1,)], near[1]), 1)
    sums[0] = add(2, terms[(0,)], near[0])
    steps = (*distant, 1, 0)
    owners = {p: (p, p ^ 2 if p < 2 else p ^ 1) for p in steps}
    return finish(
        [owners[p] for p in steps], rows, epochs, scale, [sums[p] for p in steps]
    )


def solution(mesh):
    nodes = mesh.shape["node"]
    assert nodes & (nodes - 1) == 0
    placed = (
        P(("grp", "node", "tm"), None),
        P("grp"),
        P(("grp", "node", "tm"), None),
        P(("grp", "node"), None, None, None),
        P(("grp", "node"), None),
        P(("grp", "node")),
    )
    return jax.shard_map(
        functools.partial(on_device, nodes),
        mesh=mesh,
        in_specs=placed,
        out_specs=P(("grp", "node", "tm"), None),
        check_vma=False,
    )
```
